32 devices in a mesh: occ: 4 (over z), vir: 8 (over y, x, core).
Axes of the slice: x: 2, y: 2, z: 4, core: 2. Of those that a mesh axis runs over, the one named last changes fastest.
Arguments:
- amplitudes: bfloat16 [40, 40, 400, 400], P('occ', None, 'vir'), may hold values from -6 to 6
- integrals: bfloat16 [400, 400, 3200], P('vir', 'occ'), may hold values from -0.109375 to 0.109375
- batch_index: int32 [1], replicated, may hold values from 0 to 49
- eps_occ: float32 [40], replicated, may hold values from -1 to -0.3
- eps_vir: float32 [400], replicated, may hold values from 0.2 to 1.5
Outputs:
- update: float32 [400, 400, 1600], P(None, 'vir', 'occ')
The draws below stay inside these ranges and needn't reach their ends.
Inputs may be any that keep to these rules, and one draw needn't show every extreme that they name: Selects the virtual orbitals d from 8 * batch_index to 8 * batch_index + 7.
All inputs are finite; a program needn't handle non-finite values.
Results may differ from the reference program's by a relative error of at most 0.0029.
Values may be sent and summed in bfloat16 or wider, within the bound.
A program may use at most 384 MiB of HBM per device.

```python
import jax
import jax.numpy as jnp
from jax import lax

OCC = 40
VIR = 400
NB = 8


def block_scale(stream_key, extent, pieces, smallest, largest):
    loudness, own = 1.0, jax.random.fold_in(stream_key, 6)
    for position, blocks in pieces:
        draws = jnp.exp(jax.random.uniform(jax.random.fold_in(own, position), (blocks,), jnp.float32, smallest / len(pieces), largest / len(pieces)))
        loudness = loudness * jnp.repeat(draws, extent[position] // blocks).reshape([-1 if axis == position else 1 for axis in range(len(extent))])
    return loudness


def noise(stream_key, dims, width, reach, shards=(), kind=jnp.bfloat16):
    values = jax.random.normal(stream_key, dims, jnp.float32) * width
    if len(shards) > 0:
        values = block_scale(stream_key, dims, shards, -0.22, 0.18) * values
    return jnp.clip(values, min=-reach, max=reach).astype(kind)


def setup_inputs(seed: int = 0) -> dict:
    splits = jax.random.split(jax.random.key(seed), 6)
    return {
        "amplitudes": noise(splits[0], (OCC, OCC, VIR, VIR), 1.0, 6.0, ((0, 4), (2, 8))),
        "integrals": noise(splits[1], (VIR, VIR, VIR * NB), (VIR * NB) ** -0.5, 0.109375, ((0, 8), (1, 4))),
        "batch_index": jax.random.randint(splits[2], (1,), 0, VIR // NB).astype(jnp.int32),
        "eps_occ": jnp.clip(jax.random.uniform(splits[3], (OCC,), jnp.float32, -1.0, -0.3), -1.0, -0.3),
        "eps_vir": jnp.clip(jax.random.uniform(splits[4], (VIR,), jnp.float32, 0.2, 1.5), 0.2, 1.5),
    }


def reference(amplitudes, integrals, batch_index, eps_occ, eps_vir):
    begin = (batch_index[0] * NB).astype(jnp.int32)
    selected = lax.dynamic_slice_in_dim(amplitudes, begin, NB, 3).reshape(OCC * OCC, VIR * NB)
    weights_flat = integrals.reshape(VIR * VIR, VIR * NB)
    ladder = 0.5 * jnp.dot(weights_flat, selected.T, preferred_element_type=jnp.float32)
    ladder = ladder.reshape(VIR, VIR, OCC, OCC)
    mixed = (ladder - jnp.transpose(ladder, (0, 1, 3, 2))).astype(jnp.bfloat16)
    mixed = mixed.reshape(VIR, VIR, OCC * OCC).astype(jnp.float32)
    pair_energy = (eps_occ[:, None] + eps_occ[None, :]).reshape(OCC * OCC)
    denominator = pair_energy[None, None, :] - eps_vir[:, None, None] - eps_vir[None, :, None]
    return (mixed - jnp.transpose(mixed, (1, 0, 2))) / denominator
```

```python
import jax
import jax.numpy as jnp
from jax import lax
from jax.sharding import PartitionSpec as P

NB = 8


def shards(amplitudes, integrals, batch_index, eps_occ, eps_vir):
    occ_rows = amplitudes.shape[0]
    occ_all = amplitudes.shape[1]
    vir_local = amplitudes.shape[2]
    block_a = integrals.shape[0]
    block_b = integrals.shape[1]
    begin = batch_index[0] * NB
    sliced = lax.dynamic_slice_in_dim(amplitudes, begin, NB, 3)
    sliced = sliced.reshape(occ_rows, occ_all, vir_local * NB)
    weights_flat = integrals.reshape(block_a * block_b, integrals.shape[2])
    dims_last = (((1,), (1,)), ((), ()))
    columns = lax.all_gather(sliced, "vir", axis=2, tiled=True)
    columns = columns.reshape(occ_rows * occ_all, columns.shape[2])
    ladder = lax.dot_general(
        weights_flat,
        lax.all_gather(columns, "occ", axis=0, tiled=True),
        dims_last,
        preferred_element_type=jnp.float32,
    )
    ladder = 0.5 * ladder.reshape(block_a, block_b, occ_all, occ_all)
    mixed = (ladder - jnp.transpose(ladder, (0, 1, 3, 2))).astype(jnp.bfloat16)
    mixed = mixed.reshape(block_a, block_b, occ_all * occ_all)
    own_rows = lax.all_to_all(mixed, "occ", split_axis=2, concat_axis=1, tiled=True)
    relaid = lax.all_to_all(own_rows, "vir", split_axis=1, concat_axis=0, tiled=True)
    mirrored = jnp.swapaxes(own_rows, 0, 1)
    pair_count = relaid.shape[2]
    pair_rows = pair_count // occ_all
    width_b = relaid.shape[1]
    occ_index = lax.axis_index("occ")
    vir_index = lax.axis_index("vir")
    energy_rows = lax.dynamic_slice_in_dim(eps_occ, occ_index * pair_rows, pair_rows, 0)
    pair_energy = (energy_rows[:, None] + eps_occ[None, :]).reshape(pair_count)
    energy_cols = lax.dynamic_slice_in_dim(eps_vir, vir_index * width_b, width_b, 0)
    denominator = pair_energy[None, None, :] - eps_vir[:, None, None] - energy_cols[None, :, None]
    return (relaid.astype(jnp.float32) - mirrored.astype(jnp.float32)) / denominator


def solution(mesh):
    in_specs = (P("occ", None, "vir", None), P("vir", "occ", None), P(), P(), P())
    out_specs = P(None, "vir", "occ")
    return jax.shard_map(shards, mesh=mesh, in_specs=in_specs, out_specs=out_specs, check_vma=False)
```

```python
import functools

import jax
import jax.numpy as jnp
import numpy as np
from jax import lax
from jax.experimental import pallas as pl
from jax.experimental.pallas import tpu as pltpu
from jax.sharding import PartitionSpec as P

NB = 8
MESH = pl.DeviceIdType.MESH
VMEM_LIMIT = 60 * 1024 * 1024


def up(value, step):
    return -(-value // step) * step


def pair_tables(occ_all, occ_ranks):
    rows = occ_all // occ_ranks
    pairs = [(i, j) for i in range(occ_all) for j in range(i + 1, occ_all)]
    place = {pair: k for k, pair in enumerate(pairs)}
    count = up(len(pairs), 16)
    first = np.zeros((count,), np.int32)
    second = np.zeros((count,), np.int32)
    for k, (i, j) in enumerate(pairs):
        first[k], second[k] = i * occ_all + j, j * occ_all + i
    width = 0
    lists = []
    for owner in range(occ_ranks):
        mine = range(owner * rows, (owner + 1) * rows)
        lists.append([p for p in pairs if p[0] in mine or p[1] in mine])
        width = max(width, len(lists[-1]))
    width = up(width, 128)
    spread = np.zeros((count, occ_ranks * width), np.float32)
    expand = np.zeros((occ_ranks, width, up(rows * occ_all, 128)), np.float32)
    for owner, owned in enumerate(lists):
        low = owner * rows
        for k, (i, j) in enumerate(owned):
            spread[place[(i, j)], owner * width + k] = 1.0
            if low <= i < low + rows:
                expand[owner, k, (i - low) * occ_all + j] = 1.0
            if low <= j < low + rows:
                expand[owner, k, (j - low) * occ_all + i] = -1.0
    return first, second, spread, expand, count, width


def ladder_kernel(group, block_b, owners, width, w_ref, s_ref, t_ref, e_ref, out_ref):
    dims = (((1,), (1,)), ((), ()))
    weights = w_ref[...]
    left = lax.dot_general(weights, s_ref[...], dims, preferred_element_type=jnp.float32)
    right = lax.dot_general(weights, t_ref[...], dims, preferred_element_type=jnp.float32)
    mixed = (0.5 * left - 0.5 * right).astype(jnp.bfloat16)
    parts = jnp.dot(mixed, e_ref[...], preferred_element_type=jnp.float32)
    for owner in range(owners):
        for a in range(group):
            piece = parts[a * block_b : (a + 1) * block_b, owner * width : (owner + 1) * width]
            out_ref[owner, a, 0:block_b, :] = piece.astype(jnp.bfloat16)


def ladder_call(weights, first, second, spread, block_a, block_b, tall, owners, width):
    group = next(g for g in range(1, block_a + 1) if block_a % g == 0 and (g == block_a or g * block_b % 8 == 0))
    depth = weights.shape[1]
    count = first.shape[0]
    once = pl.Buffered(1)
    return pl.pallas_call(
        functools.partial(ladder_kernel, group, block_b, owners, width),
        grid=(block_a // group,),
        in_specs=[
            pl.BlockSpec((group * block_b, depth), lambda g: (g, 0)),
            pl.BlockSpec((count, depth), lambda g: (0, 0), pipeline_mode=once),
            pl.BlockSpec((count, depth), lambda g: (0, 0), pipeline_mode=once),
            pl.BlockSpec((count, owners * width), lambda g: (0, 0), pipeline_mode=once),
        ],
        out_specs=pl.BlockSpec((owners, group, tall, width), lambda g: (0, g, 0, 0)),
        out_shape=jax.ShapeDtypeStruct((owners, block_a, tall, width), jnp.bfloat16),
        compiler_params=pltpu.CompilerParams(vmem_limit_bytes=VMEM_LIMIT),
    )(weights, first, second, spread)


def exchange_kernel(occ_n, vir_n, pieces, step, starts, length, m_ref, r_ref, x_ref, hold, zs, zr, vs, vr, ls):
    occ = lax.axis_index("occ")
    vir = lax.axis_index("vir")
    ratio = vir_n // occ_n
    barrier = pltpu.get_barrier_semaphore()
    for k in range(1, occ_n):
        pl.semaphore_signal(barrier, inc=1, device_id={"occ": lax.rem(occ + k, occ_n)}, device_id_type=MESH)
    for k in range(1, vir_n):
        pl.semaphore_signal(barrier, inc=1, device_id={"vir": lax.rem(vir + k, vir_n)}, device_id_type=MESH)
    pl.semaphore_wait(barrier, occ_n - 1 + vir_n - 1)

    def z_copy(k, c):
        peer = lax.rem(occ + k, occ_n)
        rows = pl.ds(c * step, step)
        return pltpu.make_async_remote_copy(
            src_ref=m_ref.at[peer, rows],
            dst_ref=r_ref.at[occ, rows],
            send_sem=zs.at[k - 1, c],
            recv_sem=zr.at[k - 1, c],
            device_id={"occ": peer},
            device_id_type=MESH,
        )

    def forward(src_ref, quarter, k, c):
        rows = pl.ds(c * step, step)
        for h in range(ratio):
            target = quarter * ratio + h
            piece = src_ref.at[quarter, rows, pl.ds(starts[h], length)]

            @pl.when(target != vir)
            def _():
                pltpu.make_async_remote_copy(
                    src_ref=piece,
                    dst_ref=x_ref.at[vir, rows],
                    send_sem=vs.at[k, h, c],
                    recv_sem=vr.at[vir, c],
                    device_id={"vir": target},
                    device_id_type=MESH,
                ).start()

            @pl.when(target == vir)
            def _():
                into = pltpu.make_async_copy(piece, hold, ls.at[0])
                into.start()
                into.wait()
                out = pltpu.make_async_copy(hold, x_ref.at[vir, rows], ls.at[1])
                out.start()
                out.wait()

    for c in range(pieces):
        for k in range(1, occ_n):
            z_copy(k, c).start()
    for c in range(pieces):
        forward(m_ref, occ, 0, c)
        for k in range(1, occ_n):
            z_copy(k, c).wait_recv()
            forward(r_ref, lax.rem(occ + occ_n - k, occ_n), k, c)
    for c in range(pieces):
        rows = pl.ds(c * step, step)
        for k in range(1, occ_n):
            z_copy(k, c).wait_send()
        for k in range(occ_n):
            quarter = lax.rem(occ + occ_n - k, occ_n)
            for h in range(ratio):
                target = quarter * ratio + h

                @pl.when(target != vir)
                def _():
                    pltpu.make_async_remote_copy(
                        src_ref=x_ref.at[vir, rows],
                        dst_ref=x_ref.at[vir, rows],
                        send_sem=vs.at[k, h, c],
                        recv_sem=vr.at[vir, c],
                        device_id={"vir": target},
                        device_id_type=MESH,
                    ).wait_send()

        for k in range(1, vir_n):
            source = lax.rem(vir + k, vir_n)
            pltpu.make_async_remote_copy(
                src_ref=x_ref.at[source, rows],
                dst_ref=x_ref.at[source, rows],
                send_sem=vs.at[0, 0, c],
                recv_sem=vr.at[source, c],
                device_id={"vir": source},
                device_id_type=MESH,
            ).wait_recv()


def exchange_call(terms, vir_n, starts, length):
    occ_n, block_a, tall, width = terms.shape
    pieces = 5
    step = block_a // pieces
    ratio = vir_n // occ_n
    anywhere = pl.BlockSpec(memory_space=pl.ANY)
    return pl.pallas_call(
        functools.partial(exchange_kernel, occ_n, vir_n, pieces, step, starts, length),
        in_specs=[anywhere],
        out_specs=[anywhere, anywhere],
        out_shape=[
            jax.ShapeDtypeStruct(terms.shape, terms.dtype),
            jax.ShapeDtypeStruct((vir_n, block_a, length, width), terms.dtype),
        ],
        scratch_shapes=[
            pltpu.VMEM((step, length, width), terms.dtype),
            pltpu.SemaphoreType.DMA((occ_n - 1, pieces)),
            pltpu.SemaphoreType.DMA((occ_n - 1, pieces)),
            pltpu.SemaphoreType.DMA((occ_n, ratio, pieces)),
            pltpu.SemaphoreType.DMA((vir_n, pieces)),
            pltpu.SemaphoreType.DMA((2,)),
        ],
        compiler_params=pltpu.CompilerParams(collective_id=0, has_side_effects=True, vmem_limit_bytes=16 * 1024 * 1024),
    )(terms)


def combine_kernel(sub, shifts, quarter_rows, where, ev_ref, m_ref, r_ref, x_ref, e_ref, pair_ref, eb_ref, out_ref, *mirror):
    k, s = pl.program_id(0), pl.program_id(1)
    count_b, tall, width = m_ref.shape[1:]
    out_b, pair_count = out_ref.shape[1:]
    expand = e_ref[...]

    def fill(ref):
        def body(b, _):
            whole = jnp.dot(ref[0, b], expand, preferred_element_type=jnp.float32)
            for n, lanes in enumerate(mirror):
                lanes[pl.ds(pl.multiple_of(b * tall, 8), tall), :] = whole[:, n * 128 : (n + 1) * 128]
            return 0

        lax.fori_loop(0, count_b, body, 0)

    @pl.when(jnp.logical_and(s == 0, k == 0))
    def _():
        fill(m_ref)

    @pl.when(jnp.logical_and(s == 0, k > 0))
    def _():
        fill(r_ref)

    base = s * sub
    half = where[1]
    first_a = (where[0] + k) % pl.num_programs(0) * quarter_rows + base

    def row(i, _):
        whole = jnp.dot(x_ref[0, i], expand, preferred_element_type=jnp.float32)
        direct = whole[shifts[0] : shifts[0] + out_b]
        for h in range(1, len(shifts)):
            direct = jnp.where(half == h, whole[shifts[h] : shifts[h] + out_b], direct)
        back = jnp.concatenate([lanes[pl.ds(base + i, out_b, stride=tall), :] for lanes in mirror], axis=1)
        denominator = pair_ref[...] - ev_ref[first_a + i] - eb_ref[...]
        out_ref[i] = (direct - back)[:, :pair_count] / denominator
        return 0

    lax.fori_loop(0, sub, row, 0)


def combine_call(where, eps_vir, terms, own, relaid, expand, pair_energy, energy_b, block_a, ratio, starts):
    occ_n, _, tall, width = terms.shape
    vir_n, _, length, _ = relaid.shape
    sub = block_a // 5
    steps = ratio * 5
    out_b = block_a
    pair_count = pair_energy.shape[1]
    lanes = expand.shape[1]
    shifts = tuple(h * out_b - starts[h] for h in range(ratio))

    def peer(k, w):
        return (w[0] + k) % occ_n

    spec = pltpu.PrefetchScalarGridSpec(
        num_scalar_prefetch=2,
        grid=(occ_n, steps),
        in_specs=[
            pl.BlockSpec((1, block_a, tall, width), lambda k, s, w, ev: (w[0], 0, 0, 0), pipeline_mode=pl.Buffered(1)),
            pl.BlockSpec((1, block_a, tall, width), lambda k, s, w, ev: (peer(jnp.maximum(k, 1), w), 0, 0, 0)),
            pl.BlockSpec((1, sub, length, width), lambda k, s, w, ev: (peer(k, w) * ratio + s // 5, s % 5, 0, 0)),
            pl.BlockSpec((width, lanes), lambda k, s, w, ev: (0, 0)),
            pl.BlockSpec((1, pair_count), lambda k, s, w, ev: (0, 0)),
            pl.BlockSpec((out_b, 1), lambda k, s, w, ev: (0, 0)),
        ],
        out_specs=pl.BlockSpec((sub, out_b, pair_count), lambda k, s, w, ev: (peer(k, w) * steps + s, 0, 0)),
        scratch_shapes=[pltpu.VMEM((block_a * tall, 128), jnp.float32)] * (lanes // 128),
    )
    return pl.pallas_call(
        functools.partial(combine_kernel, sub, shifts, ratio * block_a),
        grid_spec=spec,
        out_shape=jax.ShapeDtypeStruct((vir_n * block_a, out_b, pair_count), jnp.float32),
        compiler_params=pltpu.CompilerParams(vmem_limit_bytes=VMEM_LIMIT),
    )(where, eps_vir, terms, own, relaid, expand, pair_energy, energy_b)


def shards(occ_n, vir_n, amplitudes, integrals, batch_index, eps_occ, eps_vir):
    occ_rows, occ_all, vir_local = amplitudes.shape[:3]
    block_a, block_b, depth = integrals.shape
    ratio = block_b // block_a
    pair_count = occ_rows * occ_all
    starts = tuple(h * block_a // 8 * 8 for h in range(ratio))
    length = max(up((h + 1) * block_a, 8) - starts[h] for h in range(ratio))
    tall = max(up(block_b, 8), max(s + length for s in starts))
    first, second, spread, expand, count, width = pair_tables(occ_all, occ_n)
    occ_index = lax.axis_index("occ")
    vir_index = lax.axis_index("vir")

    sliced = lax.dynamic_slice_in_dim(amplitudes, batch_index[0] * NB, NB, 3)
    sliced = sliced.reshape(pair_count, vir_local * NB)
    columns = lax.all_gather(sliced, "occ", axis=0, tiled=True)
    selected = lax.all_gather(columns, "vir", axis=1, tiled=True)
    weights = integrals.reshape(block_a * block_b, depth)
    terms = ladder_call(
        weights,
        jnp.take(selected, first, axis=0),
        jnp.take(selected, second, axis=0),
        jnp.asarray(spread, jnp.bfloat16),
        block_a,
        block_b,
        tall,
        occ_n,
        width,
    )
    own, relaid = exchange_call(terms, vir_n, starts, length)
    energy_rows = lax.dynamic_slice_in_dim(eps_occ, occ_index * occ_rows, occ_rows, 0)
    pair_energy = (energy_rows[:, None] + eps_occ[None, :]).reshape(1, pair_count)
    energy_b = lax.dynamic_slice_in_dim(eps_vir, vir_index * block_a, block_a, 0).reshape(block_a, 1)
    mine = lax.dynamic_index_in_dim(jnp.asarray(expand, jnp.bfloat16), occ_index, 0, keepdims=False)
    where = jnp.stack([occ_index, vir_index % ratio]).astype(jnp.int32)
    return combine_call(where, eps_vir, terms, own, relaid, mine, pair_energy, energy_b, block_a, ratio, starts)


def solution(mesh):
    in_specs = (P("occ", None, "vir", None), P("vir", "occ", None), P(), P(), P())
    out_specs = P(None, "vir", "occ")
    body = functools.partial(shards, mesh.shape["occ"], mesh.shape["vir"])
    return jax.shard_map(body, mesh=mesh, in_specs=in_specs, out_specs=out_specs, check_vma=False)
```
